32 devices in a mesh: fsdp: 32 (over z, y, x, core).
Axes of the slice: x: 2, y: 2, z: 4, core: 2. Of those that a mesh axis runs over, the one named last changes fastest.
Arguments:
- images: bfloat16 [64, 81, 768], P('fsdp'), may hold values from -6 to 6
- cotangent: bfloat16 [64, 81, 768], P('fsdp'), may hold values from -6 to 6
- image_count: int32 [32], P('fsdp'), may hold values from 1 to 2, as said below
- ln1_gain: bfloat16 [768], P('fsdp'), may hold values from 0.5 to 1.5
- ln1_shift: bfloat16 [768], P('fsdp'), may hold values from -3 to 3
- w_qkv: bfloat16 [768, 2304], P('fsdp'), may hold values from -0.21875 to 0.21875
- q_bias: bfloat16 [768], P('fsdp'), may hold values from -3 to 3
- v_bias: bfloat16 [768], P('fsdp'), may hold values from -3 to 3
- w_out: bfloat16 [768, 768], P('fsdp'), may hold values from -0.625 to 0.625
- out_bias: bfloat16 [768], P('fsdp'), may hold values from -3 to 3
- ln2_gain: bfloat16 [768], P('fsdp'), may hold values from 0.5 to 1.5
- ln2_shift: bfloat16 [768], P('fsdp'), may hold values from -3 to 3
- w_up: bfloat16 [768, 3072], P('fsdp'), may hold values from -0.21875 to 0.21875
- up_bias: bfloat16 [3072], P('fsdp'), may hold values from -3 to 3
- w_down: bfloat16 [3072, 768], P('fsdp'), may hold values from -0.109375 to 0.109375
- down_bias: bfloat16 [768], P('fsdp'), may hold values from -3 to 3
Outputs:
- layer_out: bfloat16 [64, 81, 768], P('fsdp')
- grad_images: float32 [64, 81, 768], P('fsdp')
- grad_ln1_gain: float32 [768], P('fsdp')
- grad_ln1_shift: float32 [768], P('fsdp')
- grad_w_qkv: float32 [768, 2304], P('fsdp')
- grad_q_bias: float32 [768], P('fsdp')
- grad_v_bias: float32 [768], P('fsdp')
- grad_w_out: float32 [768, 768], P('fsdp')
- grad_out_bias: float32 [768], P('fsdp')
- grad_ln2_gain: float32 [768], P('fsdp')
- grad_ln2_shift: float32 [768], P('fsdp')
- grad_w_up: float32 [768, 3072], P('fsdp')
- grad_up_bias: float32 [3072], P('fsdp')
- grad_w_down: float32 [3072, 768], P('fsdp')
- grad_down_bias: float32 [768], P('fsdp')
The draws below stay inside these ranges and needn't reach their ends.
Inputs may be any that keep to these rules, and one draw needn't show every extreme that they name: The first image_count[d] of device d's 2 slots hold images; some device has all 2 live and some only 1.
All inputs are finite; a program needn't handle non-finite values.
Results may differ from the reference program's by a relative error of at most 0.014.
Values may be sent and summed in bfloat16 or wider, within the bound.
No kernel may reach another device: no remote copies, remote signals or barrier semaphores. Data moves between devices by JAX's collectives and lax.ppermute only.
A program may use at most 192 MiB of HBM per device.

```python
import jax
import jax.numpy as jnp
from jax import lax

D = 768
HEAD_DIM = 64
FF = 3072
TOK = 81
SLOTS = 2
IMAGES = 64
N_FSDP = 32


def draw_image_count(key, part):
    first_key = jax.random.fold_in(key, 11)
    second_key = jax.random.fold_in(key, 23)
    lowest = SLOTS // 2
    counts = jax.random.randint(first_key, (N_FSDP,), lowest, SLOTS + 1)
    order = jax.random.permutation(second_key, N_FSDP)
    counts = counts.at[order[0]].set(SLOTS)
    counts = counts.at[order[1]].set(lowest)
    return counts.astype(jnp.int32)


def with_spikes(drawn, rng, source, target, blocks, factor):
    owner, partner = [(jnp.arange(drawn.shape[position]) // (drawn.shape[position] // blocks)).reshape([-1 if axis == position else 1 for axis in range(drawn.ndim)]) for position in (source, target)]
    chosen = jax.random.permutation(rng, blocks)[partner]
    strong = (owner == chosen) | (owner == (partner + blocks // 2) % blocks)
    return jnp.where(strong, factor * drawn, drawn)


def steps_of(own_key, shape, pieces, smallest, high):
    def one(position, shards_of):
        steps = jax.random.uniform(jax.random.fold_in(jax.random.fold_in(own_key, 6), position), (shards_of,), jnp.float32, smallest / len(pieces), high / len(pieces))
        return jnp.repeat(jnp.exp(steps), shape[position] // shards_of).reshape((-1,) + (1,) * (len(shape) - position - 1))

    level = one(*pieces[0])
    for cut in pieces[1:]:
        level = level * one(*cut)
    return level


def noise(rng, extent, spread, limit, shards=(), kind=jnp.bfloat16):
    entries = jax.random.normal(rng, extent, jnp.float32) * spread
    if len(shards) > 0:
        entries = steps_of(rng, extent, shards, -0.22, 0.18) * entries
    return jnp.clip(entries, min=-limit, max=limit).astype(kind)


def heavy_noise(rng, shape, width, reach, shards, heavy, kind=jnp.bfloat16):
    result = width * jax.random.normal(rng, shape, jnp.float32)
    if shards:
        result = result * steps_of(rng, shape, shards, -0.22, 0.18)
    return jnp.clip(with_spikes(result, jax.random.fold_in(rng, 3), *heavy), -reach, reach).astype(kind)


def setup_inputs(seed: int = 0) -> dict:
    arg_keys = jax.random.split(jax.random.key(seed), 17)
    images = heavy_noise(arg_keys[0], (IMAGES, TOK, D), 1.0, 6.0, ((0, 32),), (0, 2, 32, 2.75))
    cotangent = noise(arg_keys[1], (IMAGES, TOK, D), 1.0, 6.0, ((0, 32),))
    image_count = draw_image_count(jax.random.fold_in(arg_keys[16], 71), 0)
    ln1_gain = jnp.clip(1.0 + 0.1 * jax.random.normal(arg_keys[3], (D,), jnp.float32), 0.5, 1.5).astype(jnp.bfloat16)
    ln1_shift = noise(arg_keys[4], (D,), 0.5, 3.0, ((0, 32),))
    w_qkv = noise(arg_keys[5], (D, 3 * D), D ** -0.5, 0.21875, ((0, 32),))
    q_bias = noise(arg_keys[6], (D,), 0.5, 3.0, ((0, 32),))
    v_bias = noise(arg_keys[7], (D,), 0.5, 3.0, ((0, 32),))
    w_out = noise(arg_keys[8], (D, D), (D // 8) ** -0.5, 0.625, ((0, 32),))
    out_bias = noise(arg_keys[9], (D,), 0.5, 3.0, ((0, 32),))
    ln2_gain = jnp.clip(1.0 + 0.1 * jax.random.normal(arg_keys[10], (D,), jnp.float32), 0.5, 1.5).astype(jnp.bfloat16)
    ln2_shift = noise(arg_keys[11], (D,), 0.5, 3.0, ((0, 32),))
    w_up = noise(arg_keys[12], (D, FF), D ** -0.5, 0.21875, ((0, 32),))
    up_bias = noise(arg_keys[13], (FF,), 0.5, 3.0, ((0, 32),))
    w_down = noise(arg_keys[14], (FF, D), FF ** -0.5, 0.109375, ((0, 32),))
    down_bias = noise(arg_keys[15], (D,), 0.5, 3.0, ((0, 32),))
    return {"images": images, "cotangent": cotangent, "image_count": image_count, "ln1_gain": ln1_gain, "ln1_shift": ln1_shift, "w_qkv": w_qkv, "q_bias": q_bias, "v_bias": v_bias, "w_out": w_out, "out_bias": out_bias, "ln2_gain": ln2_gain, "ln2_shift": ln2_shift, "w_up": w_up, "up_bias": up_bias, "w_down": w_down, "down_bias": down_bias}


EPS = 1e-06
SQRT_HALF = 0.7071067811865476
INV_ROOT_TWO_PI = 0.3989422804014327

def outer_sum(left_mat, right_mat):
    return lax.dot_general(left_mat, right_mat, (((0,), (0,)), ((), ())), preferred_element_type=jnp.float32)

def back_product(left_mat, weight_mat):
    return lax.dot_general(left_mat, weight_mat, (((1,), (1,)), ((), ())), preferred_element_type=jnp.float32)

def norm_forward(features, gain_vec, shift_vec):
    row_mean = lax.optimization_barrier(jnp.mean(features, axis=-1, keepdims=True))
    centered = features - row_mean
    inverse = lax.rsqrt(lax.optimization_barrier(jnp.mean(centered * centered, axis=-1, keepdims=True)) + EPS)
    normed = centered * inverse
    return (normed, inverse, normed * gain_vec.astype(jnp.float32) + shift_vec.astype(jnp.float32))

def norm_backward(grad_norm, normed, inverse, gain_vec):
    scaled = grad_norm * gain_vec.astype(jnp.float32)
    return inverse * (scaled - lax.optimization_barrier(jnp.mean(scaled, axis=-1, keepdims=True)) - normed * lax.optimization_barrier(jnp.mean(scaled * normed, axis=-1, keepdims=True)))

def layer_forward(params, image_block, live_block):
    ln1_gain, ln1_shift, w_qkv, q_bias, v_bias, w_out, out_bias, ln2_gain, ln2_shift, w_up, up_bias, w_down, down_bias = params
    num_images, num_tokens, feat_width = image_block.shape
    num_heads = feat_width // HEAD_DIM
    head_scale = HEAD_DIM ** (-0.5)
    row_mask = jnp.repeat(live_block.astype(jnp.float32), num_tokens)[:, None]
    flat_rows = image_block.reshape(num_images * num_tokens, feat_width).astype(jnp.float32)
    normed1, inverse1, pre_one = norm_forward(flat_rows, ln1_gain, ln1_shift)
    act_one = pre_one.astype(jnp.bfloat16)
    qkv_all = jnp.dot(act_one, w_qkv, preferred_element_type=jnp.float32)
    queries = ((qkv_all[:, :feat_width] + q_bias.astype(jnp.float32)) * head_scale).astype(jnp.bfloat16)
    key_rows = qkv_all[:, feat_width:2 * feat_width].astype(jnp.bfloat16)
    value_rows = (qkv_all[:, 2 * feat_width:] + v_bias.astype(jnp.float32)).astype(jnp.bfloat16)
    query_heads = queries.reshape(num_images, num_tokens, num_heads, HEAD_DIM)
    key_heads = key_rows.reshape(num_images, num_tokens, num_heads, HEAD_DIM)
    value_heads = value_rows.reshape(num_images, num_tokens, num_heads, HEAD_DIM)
    scores = jnp.einsum('bqhd,bkhd->bhqk', query_heads, key_heads, preferred_element_type=jnp.float32)
    row_top = lax.optimization_barrier(jnp.max(scores, axis=-1, keepdims=True))
    exp_scores = jnp.exp(scores - row_top)
    exp_total = lax.optimization_barrier(jnp.sum(exp_scores, axis=-1, keepdims=True))
    log_total = row_top + jnp.log(exp_total)
    prob_bf = (exp_scores / exp_total).astype(jnp.bfloat16)
    mixed_heads = jnp.einsum('bhqk,bkhd->bqhd', prob_bf, value_heads, preferred_element_type=jnp.float32)
    attn_rows = mixed_heads.reshape(num_images * num_tokens, feat_width).astype(jnp.bfloat16)
    hidden = flat_rows + jnp.dot(attn_rows, w_out, preferred_element_type=jnp.float32) + out_bias.astype(jnp.float32)
    normed2, inverse2, pre_two = norm_forward(hidden, ln2_gain, ln2_shift)
    act_two = pre_two.astype(jnp.bfloat16)
    pre_gelu = jnp.dot(act_two, w_up, preferred_element_type=jnp.float32) + up_bias.astype(jnp.float32)
    act_three = (pre_gelu * 0.5 * (1.0 + jax.scipy.special.erf(pre_gelu * SQRT_HALF))).astype(jnp.bfloat16)
    down_rows = jnp.dot(act_three, w_down, preferred_element_type=jnp.float32) + down_bias.astype(jnp.float32)
    block_out = ((hidden + down_rows) * row_mask).astype(jnp.bfloat16).reshape(num_images, num_tokens, feat_width)
    saved_state = (normed1, inverse1, act_one, query_heads, key_heads, value_heads, log_total, mixed_heads, attn_rows, normed2, inverse2, act_two, pre_gelu, act_three, row_mask)
    return (block_out, saved_state)

def layer_backward(params, saved_state, cot_block):
    ln1_gain, ln1_shift, w_qkv, q_bias, v_bias, w_out, out_bias, ln2_gain, ln2_shift, w_up, up_bias, w_down, down_bias = params
    normed1, inverse1, act_one, query_heads, key_heads, value_heads, log_total, mixed_heads, attn_rows, normed2, inverse2, act_two, pre_gelu, act_three, row_mask = saved_state
    num_images, num_tokens, feat_width = cot_block.shape
    head_scale = HEAD_DIM ** (-0.5)
    grad_rows = cot_block.reshape(num_images * num_tokens, feat_width).astype(jnp.float32) * row_mask
    grad_bf = grad_rows.astype(jnp.bfloat16)
    grad_down_bias = lax.optimization_barrier(jnp.sum(grad_rows, axis=0))
    grad_w_down = outer_sum(act_three, grad_bf)
    grad_three = back_product(grad_bf, w_down)
    slope = 0.5 * (1.0 + jax.scipy.special.erf(pre_gelu * SQRT_HALF)) + pre_gelu * INV_ROOT_TWO_PI * jnp.exp(-0.5 * pre_gelu * pre_gelu)
    grad_pre = grad_three * slope
    grad_up_bias = lax.optimization_barrier(jnp.sum(grad_pre, axis=0))
    grad_pre_bf = grad_pre.astype(jnp.bfloat16)
    grad_w_up = outer_sum(act_two, grad_pre_bf)
    grad_two = back_product(grad_pre_bf, w_up)
    grad_ln2_gain = lax.optimization_barrier(jnp.sum(grad_two * normed2, axis=0))
    grad_ln2_shift = lax.optimization_barrier(jnp.sum(grad_two, axis=0))
    grad_hidden = grad_rows + norm_backward(grad_two, normed2, inverse2, ln2_gain)
    grad_out_bias = lax.optimization_barrier(jnp.sum(grad_hidden, axis=0))
    grad_hidden_bf = grad_hidden.astype(jnp.bfloat16)
    grad_w_out = outer_sum(attn_rows, grad_hidden_bf)
    grad_attn = back_product(grad_hidden_bf, w_out).astype(jnp.bfloat16)
    grad_attn_heads = grad_attn.reshape(mixed_heads.shape)
    scores = jnp.einsum('bqhd,bkhd->bhqk', query_heads, key_heads, preferred_element_type=jnp.float32)
    prob_again = jnp.exp(scores - log_total)
    prob_again_bf = prob_again.astype(jnp.bfloat16)
    grad_values = jnp.einsum('bhqk,bqhd->bkhd', prob_again_bf, grad_attn_heads, preferred_element_type=jnp.float32)
    grad_probs = jnp.einsum('bqhd,bkhd->bhqk', grad_attn_heads, value_heads, preferred_element_type=jnp.float32)
    row_delta = jnp.einsum('bqhd,bqhd->bhq', grad_attn_heads.astype(jnp.float32), mixed_heads)
    grad_scores = (prob_again * (grad_probs - row_delta[..., None])).astype(jnp.bfloat16)
    grad_queries = jnp.einsum('bhqk,bkhd->bqhd', grad_scores, key_heads, preferred_element_type=jnp.float32) * head_scale
    grad_keys = jnp.einsum('bhqk,bqhd->bkhd', grad_scores, query_heads, preferred_element_type=jnp.float32)
    flat_count = num_images * num_tokens
    grad_queries = grad_queries.reshape(flat_count, feat_width)
    grad_keys = grad_keys.reshape(flat_count, feat_width)
    grad_values = grad_values.reshape(flat_count, feat_width)
    grad_q_bias = lax.optimization_barrier(jnp.sum(grad_queries, axis=0))
    grad_v_bias = lax.optimization_barrier(jnp.sum(grad_values, axis=0))
    grad_qkv = jnp.concatenate([grad_queries, grad_keys, grad_values], axis=1).astype(jnp.bfloat16)
    grad_w_qkv = outer_sum(act_one, grad_qkv)
    grad_one = back_product(grad_qkv, w_qkv)
    grad_ln1_gain = lax.optimization_barrier(jnp.sum(grad_one * normed1, axis=0))
    grad_ln1_shift = lax.optimization_barrier(jnp.sum(grad_one, axis=0))
    grad_input = grad_hidden + norm_backward(grad_one, normed1, inverse1, ln1_gain)
    weight_grads = (grad_ln1_gain, grad_ln1_shift, grad_w_qkv, grad_q_bias, grad_v_bias, grad_w_out, grad_out_bias, grad_ln2_gain, grad_ln2_shift, grad_w_up, grad_up_bias, grad_w_down, grad_down_bias)
    return (grad_input.reshape(num_images, num_tokens, feat_width), weight_grads)

def reference(images, cotangent, image_count, ln1_gain, ln1_shift, w_qkv, q_bias, v_bias, w_out, out_bias, ln2_gain, ln2_shift, w_up, up_bias, w_down, down_bias):
    params = (ln1_gain, ln1_shift, w_qkv, q_bias, v_bias, w_out, out_bias, ln2_gain, ln2_shift, w_up, up_bias, w_down, down_bias)
    slot_ids = jnp.arange(N_FSDP * SLOTS, dtype=jnp.int32)
    live_all = slot_ids % SLOTS < jnp.repeat(image_count, SLOTS)
    image_blocks = images.reshape(N_FSDP, SLOTS, TOK, D)
    cot_blocks = cotangent.reshape(N_FSDP, SLOTS, TOK, D)
    live_blocks = live_all.reshape(N_FSDP, SLOTS)

    def block_step(running, inputs):
        image_block, cot_block, live_block = inputs
        block_out, saved_state = layer_forward(params, image_block, live_block)
        grad_input, weight_grads = layer_backward(params, saved_state, cot_block)
        running = tuple((left_part + right_part for left_part, right_part in zip(running, weight_grads)))
        return (running, (block_out, grad_input))
    zero_grads = tuple((jnp.zeros(param.shape, jnp.float32) for param in params))
    totals, (outputs, grad_inputs) = lax.scan(block_step, zero_grads, (image_blocks, cot_blocks, live_blocks))
    return (outputs.reshape(images.shape), grad_inputs.reshape(images.shape), totals[0], totals[1], totals[2], totals[3], totals[4], totals[5], totals[6], totals[7], totals[8], totals[9], totals[10], totals[11], totals[12])
```

```python
import jax
import jax.numpy as jnp
import numpy as np
from jax import lax
from jax.experimental import pallas as pl
from jax.experimental.pallas import tpu as pltpu
from jax.sharding import PartitionSpec as P

HEAD_DIM = 64


EPS = 1e-06
SQRT_HALF = 0.7071067811865476
INV_ROOT_TWO_PI = 0.3989422804014327


def partner(block, axis, apart):
    count = lax.axis_size(axis)
    route = []
    for low in range(count):
        high = low | 1 << apart
        if high != low and high < count:
            route += [(low, high), (high, low)]
    return lax.ppermute(block, axis, route)


def outer_sum(left_mat, right_mat):
    return lax.dot_general(
        left_mat, right_mat, (((0,), (0,)), ((), ())), preferred_element_type=jnp.float32
    )


def back_product(left_mat, weight_mat):
    return lax.dot_general(
        left_mat, weight_mat, (((1,), (1,)), ((), ())), preferred_element_type=jnp.float32
    )


def norm_forward(features, gain_vec, shift_vec):
    row_mean = jnp.mean(features, axis=-1, keepdims=True)
    centered = features - row_mean
    inverse = lax.rsqrt(jnp.mean(centered * centered, axis=-1, keepdims=True) + EPS)
    normed = centered * inverse
    return (normed, inverse, normed * gain_vec.astype(jnp.float32) + shift_vec.astype(jnp.float32))


def norm_backward(grad_norm, normed, inverse, gain_vec):
    scaled = grad_norm * gain_vec.astype(jnp.float32)
    return inverse * (
        scaled
        - jnp.mean(scaled, axis=-1, keepdims=True)
        - normed * jnp.mean(scaled * normed, axis=-1, keepdims=True)
    )


def layer_forward(params, image_block, live_block):
    (
        ln1_gain,
        ln1_shift,
        w_qkv,
        q_bias,
        v_bias,
        w_out,
        out_bias,
        ln2_gain,
        ln2_shift,
        w_up,
        up_bias,
        w_down,
        down_bias,
    ) = params
    num_images, num_tokens, feat_width = image_block.shape
    num_heads = feat_width // HEAD_DIM
    head_scale = HEAD_DIM ** (-0.5)
    row_mask = jnp.repeat(live_block.astype(jnp.float32), num_tokens)[:, None]
    flat_rows = image_block.reshape(num_images * num_tokens, feat_width).astype(jnp.float32)
    normed1, inverse1, pre_one = norm_forward(flat_rows, ln1_gain, ln1_shift)
    act_one = pre_one.astype(jnp.bfloat16)
    qkv_all = jnp.dot(act_one, w_qkv, preferred_element_type=jnp.float32)
    queries = ((qkv_all[:, :feat_width] + q_bias.astype(jnp.float32)) * head_scale).astype(
        jnp.bfloat16
    )
    key_rows = qkv_all[:, feat_width : 2 * feat_width].astype(jnp.bfloat16)
    value_rows = (qkv_all[:, 2 * feat_width :] + v_bias.astype(jnp.float32)).astype(jnp.bfloat16)
    query_heads = queries.reshape(num_images, num_tokens, num_heads, HEAD_DIM)
    key_heads = key_rows.reshape(num_images, num_tokens, num_heads, HEAD_DIM)
    value_heads = value_rows.reshape(num_images, num_tokens, num_heads, HEAD_DIM)
    scores = jnp.einsum(
        "bqhd,bkhd->bhqk", query_heads, key_heads, preferred_element_type=jnp.float32
    )
    row_top = jnp.max(scores, axis=-1, keepdims=True)
    exp_scores = jnp.exp(scores - row_top)
    exp_total = jnp.sum(exp_scores, axis=-1, keepdims=True)
    log_total = row_top + jnp.log(exp_total)
    prob_bf = (exp_scores / exp_total).astype(jnp.bfloat16)
    mixed_heads = jnp.einsum(
        "bhqk,bkhd->bqhd", prob_bf, value_heads, preferred_element_type=jnp.float32
    )
    attn_rows = mixed_heads.reshape(num_images * num_tokens, feat_width).astype(jnp.bfloat16)
    hidden = (
        flat_rows
        + jnp.dot(attn_rows, w_out, preferred_element_type=jnp.float32)
        + out_bias.astype(jnp.float32)
    )
    normed2, inverse2, pre_two = norm_forward(hidden, ln2_gain, ln2_shift)
    act_two = pre_two.astype(jnp.bfloat16)
    pre_gelu = jnp.dot(act_two, w_up, preferred_element_type=jnp.float32) + up_bias.astype(
        jnp.float32
    )
    act_three = (pre_gelu * 0.5 * (1.0 + jax.scipy.special.erf(pre_gelu * SQRT_HALF))).astype(
        jnp.bfloat16
    )
    down_rows = jnp.dot(act_three, w_down, preferred_element_type=jnp.float32) + down_bias.astype(
        jnp.float32
    )
    block_out = (
        ((hidden + down_rows) * row_mask)
        .astype(jnp.bfloat16)
        .reshape(num_images, num_tokens, feat_width)
    )
    saved_state = (
        normed1,
        inverse1,
        act_one,
        query_heads,
        key_heads,
        value_heads,
        log_total,
        mixed_heads,
        attn_rows,
        normed2,
        inverse2,
        act_two,
        pre_gelu,
        act_three,
        row_mask,
    )
    return (block_out, saved_state)


def layer_backward(params, saved_state, cot_block, products=False):
    weight_product = (lambda left, right: (left, right)) if products else outer_sum
    (
        ln1_gain,
        ln1_shift,
        w_qkv,
        q_bias,
        v_bias,
        w_out,
        out_bias,
        ln2_gain,
        ln2_shift,
        w_up,
        up_bias,
        w_down,
        down_bias,
    ) = params
    (
        normed1,
        inverse1,
        act_one,
        query_heads,
        key_heads,
        value_heads,
        log_total,
        mixed_heads,
        attn_rows,
        normed2,
        inverse2,
        act_two,
        pre_gelu,
        act_three,
        row_mask,
    ) = saved_state
    num_images, num_tokens, feat_width = cot_block.shape
    head_scale = HEAD_DIM ** (-0.5)
    grad_rows = (
        cot_block.reshape(num_images * num_tokens, feat_width).astype(jnp.float32) * row_mask
    )
    grad_bf = grad_rows.astype(jnp.bfloat16)
    grad_down_bias = jnp.sum(grad_rows, axis=0)
    grad_w_down = weight_product(act_three, grad_bf)
    grad_three = back_product(grad_bf, w_down)
    slope = 0.5 * (
        1.0 + jax.scipy.special.erf(pre_gelu * SQRT_HALF)
    ) + pre_gelu * INV_ROOT_TWO_PI * jnp.exp(-0.5 * pre_gelu * pre_gelu)
    grad_pre = grad_three * slope
    grad_up_bias = jnp.sum(grad_pre, axis=0)
    grad_pre_bf = grad_pre.astype(jnp.bfloat16)
    grad_w_up = weight_product(act_two, grad_pre_bf)
    grad_two = back_product(grad_pre_bf, w_up)
    grad_ln2_gain = jnp.sum(grad_two * normed2, axis=0)
    grad_ln2_shift = jnp.sum(grad_two, axis=0)
    grad_hidden = grad_rows + norm_backward(grad_two, normed2, inverse2, ln2_gain)
    grad_out_bias = jnp.sum(grad_hidden, axis=0)
    grad_hidden_bf = grad_hidden.astype(jnp.bfloat16)
    grad_w_out = weight_product(attn_rows, grad_hidden_bf)
    grad_attn = back_product(grad_hidden_bf, w_out).astype(jnp.bfloat16)
    grad_attn_heads = grad_attn.reshape(mixed_heads.shape)
    scores = jnp.einsum(
        "bqhd,bkhd->bhqk", query_heads, key_heads, preferred_element_type=jnp.float32
    )
    prob_again = jnp.exp(scores - log_total)
    prob_again_bf = prob_again.astype(jnp.bfloat16)
    grad_values = jnp.einsum(
        "bhqk,bqhd->bkhd", prob_again_bf, grad_attn_heads, preferred_element_type=jnp.float32
    )
    grad_probs = jnp.einsum(
        "bqhd,bkhd->bhqk", grad_attn_heads, value_heads, preferred_element_type=jnp.float32
    )
    row_delta = jnp.einsum("bqhd,bqhd->bhq", grad_attn_heads.astype(jnp.float32), mixed_heads)
    grad_scores = (prob_again * (grad_probs - row_delta[..., None])).astype(jnp.bfloat16)
    grad_queries = (
        jnp.einsum("bhqk,bkhd->bqhd", grad_scores, key_heads, preferred_element_type=jnp.float32)
        * head_scale
    )
    grad_keys = jnp.einsum(
        "bhqk,bqhd->bkhd", grad_scores, query_heads, preferred_element_type=jnp.float32
    )
    flat_count = num_images * num_tokens
    grad_queries = grad_queries.reshape(flat_count, feat_width)
    grad_keys = grad_keys.reshape(flat_count, feat_width)
    grad_values = grad_values.reshape(flat_count, feat_width)
    grad_q_bias = jnp.sum(grad_queries, axis=0)
    grad_v_bias = jnp.sum(grad_values, axis=0)
    grad_qkv = jnp.concatenate([grad_queries, grad_keys, grad_values], axis=1).astype(jnp.bfloat16)
    grad_w_qkv = weight_product(act_one, grad_qkv)
    grad_one = back_product(grad_qkv, w_qkv)
    grad_ln1_gain = jnp.sum(grad_one * normed1, axis=0)
    grad_ln1_shift = jnp.sum(grad_one, axis=0)
    grad_input = grad_hidden + norm_backward(grad_one, normed1, inverse1, ln1_gain)
    weight_grads = (
        grad_ln1_gain,
        grad_ln1_shift,
        grad_w_qkv,
        grad_q_bias,
        grad_v_bias,
        grad_w_out,
        grad_out_bias,
        grad_ln2_gain,
        grad_ln2_shift,
        grad_w_up,
        grad_up_bias,
        grad_w_down,
        grad_down_bias,
    )
    return (grad_input.reshape(num_images, num_tokens, feat_width), weight_grads)


def owner_sums(grads):
    device_count = lax.axis_size("fsdp")
    level_count = device_count.bit_length() - 1
    my_index = lax.axis_index("fsdp")
    widths = [grad.size // device_count for grad in grads]
    flat_parts = jnp.concatenate(
        [grad.reshape(device_count, grad.size // device_count) for grad in grads], axis=1
    )
    for level in range(level_count - 1, -1, -1):
        my_bit = my_index >> level & 1
        halves = flat_parts.reshape((2, flat_parts.shape[0] // 2, flat_parts.shape[1]))
        kept = jnp.where(my_bit == 0, halves[0], halves[1])
        sent = jnp.where(my_bit == 0, halves[1], halves[0])
        received = partner(sent.astype(jnp.bfloat16), "fsdp", level).astype(sent.dtype)
        flat_parts = kept + received
    flat_row = flat_parts[0]
    shards = []
    offset = 0
    for grad, width in zip(grads, widths):
        piece = flat_row[offset : offset + width]
        shards.append(piece.reshape((grad.shape[0] // device_count,) + grad.shape[1:]))
        offset = offset + width
    return tuple(shards)


AXIS = "fsdp"
PLANNED = 32


def place(index):
    return (index >> 3, index >> 2 & 1, index >> 1 & 1, index & 1)


def index_of(z, y, x, core):
    return z * 8 + y * 4 + x * 2 + core


def route(move):
    pairs = []
    for index in range(PLANNED):
        target = move(*place(index))
        if target is not None:
            pairs.append((index, index_of(*target)))
    return pairs


Z_PAIR = route(lambda z, y, x, c: (z ^ 1, y, x, c))
Z_MIDDLE = route(lambda z, y, x, c: (3 - z, y, x, c) if z in (1, 2) else None)
Z_OUT = route(lambda z, y, x, c: ({1: 0, 2: 3}[z], y, x, c) if z in (1, 2) else None)
Z_IN = route(lambda z, y, x, c: ({0: 1, 3: 2}[z], y, x, c) if z in (0, 3) else None)
NEAR = route(lambda z, y, x, c: (z, y, x ^ 1, c) if c == 0 else (z, y ^ 1, x, c))
FAR = route(lambda z, y, x, c: (z, y ^ 1, x, c) if c == 0 else (z, y, x ^ 1, c))
CORE = route(lambda z, y, x, c: (z, y, x, c ^ 1))


def block_owner(index, block, slot):
    z, y, x, core = place(index)
    plane = (z, z ^ 1, 2 if z < 2 else 1, 3 if z < 2 else 0)[slot]
    far_core, far, near = (block >> 2, block >> 1 & 1, block & 1)
    if core ^ far_core == 0:
        return index_of(plane, y ^ far, x ^ near, core ^ far_core)
    return index_of(plane, y ^ near, x ^ far, core ^ far_core)


def owner_table():
    table = [
        [block_owner(index, block, slot) for block in range(8) for slot in range(4)]
        for index in range(PLANNED)
    ]
    return np.asarray(table, dtype=np.int32)


def send(block, pairs):
    return lax.ppermute(block, AXIS, pairs)


def in_middle():
    plane = lax.axis_index(AXIS) >> 3
    return (plane == 1) | (plane == 2)


def gather_blocks(own):
    middle = in_middle()
    pair = send(own, Z_PAIR)
    cross = send(own, Z_MIDDLE)
    cross_out = send(cross, Z_OUT)
    pair_cross = send(pair, Z_MIDDLE)
    pair_cross_out = send(pair_cross, Z_OUT)
    column = jnp.stack(
        [
            own,
            pair,
            jnp.where(middle, cross, cross_out),
            jnp.where(middle, pair_cross, pair_cross_out),
        ]
    )
    near = send(column, NEAR)
    mine = [column, near, send(column, FAR), send(near, FAR)]
    return mine + [send(part, CORE) for part in mine]


def assemble_kernel(owner_ref, *refs):
    parts, whole_ref, sems = refs[:8], refs[8], refs[9]
    copies = []
    for block in range(8):
        for slot in range(4):
            spot = block * 4 + slot
            copy = pltpu.make_async_copy(
                parts[block].at[slot], whole_ref.at[owner_ref[spot]], sems.at[spot]
            )
            copy.start()
            copies.append(copy)
    for copy in copies:
        copy.wait()


def assemble(parts, owners):
    _, rows, width = parts[0].shape
    whole = pl.pallas_call(
        assemble_kernel,
        out_shape=jax.ShapeDtypeStruct((PLANNED, rows, width), parts[0].dtype),
        grid_spec=pltpu.PrefetchScalarGridSpec(
            num_scalar_prefetch=1,
            grid=(),
            in_specs=[pl.BlockSpec(memory_space=pl.ANY)] * 8,
            out_specs=pl.BlockSpec(memory_space=pltpu.VMEM),
            scratch_shapes=[pltpu.SemaphoreType.DMA((PLANNED,))],
        ),
        name="assemble",
    )(owners, *parts)
    return whole.reshape(PLANNED * rows, width)


def grad_kernel(rows, owner_ref, *refs):
    if len(refs) == 7:
        left_ref, right_ref, extra_ref, keep_ref, give_ref, made_ref, sems = refs
    else:
        left_ref, right_ref, keep_ref, give_ref, made_ref, sems = refs
        extra_ref = None
    width = right_ref.shape[1]
    span = 384
    per_span = span // rows
    right = right_ref[...]
    for step in range(left_ref.shape[1] // span):
        product = lax.dot_general(
            left_ref[:, step * span : (step + 1) * span],
            right,
            (((0,), (0,)), ((), ())),
            preferred_element_type=jnp.float32,
        ).astype(jnp.bfloat16)
        for part in range(per_span):
            owner = step * per_span + part
            made_ref[owner, :, :width] = product[part * rows : (part + 1) * rows]
            if extra_ref is not None:
                made_ref[owner, :, width:] = extra_ref[owner]
    copies = []
    for block in range(8):
        target = keep_ref if block < 4 else give_ref
        for slot in range(4):
            spot = block * 4 + slot
            copy = pltpu.make_async_copy(
                made_ref.at[owner_ref[spot]], target.at[block & 3, slot], sems.at[spot]
            )
            copy.start()
            copies.append(copy)
    for copy in copies:
        copy.wait()


def grad_blocks(owners, left, right, extra=None):
    rows = left.shape[1] // PLANNED
    width = right.shape[1] + (0 if extra is None else extra.shape[2])
    half = jax.ShapeDtypeStruct((4, 4, rows, width), jnp.bfloat16)
    operands = (left, right) if extra is None else (left, right, extra)
    return pl.pallas_call(
        lambda *refs: grad_kernel(rows, *refs),
        out_shape=(half, half),
        grid_spec=pltpu.PrefetchScalarGridSpec(
            num_scalar_prefetch=1,
            grid=(),
            in_specs=[pl.BlockSpec(memory_space=pltpu.VMEM)] * len(operands),
            out_specs=[pl.BlockSpec(memory_space=pl.ANY)] * 2,
            scratch_shapes=[
                pltpu.VMEM((PLANNED, rows, width), jnp.bfloat16),
                pltpu.SemaphoreType.DMA((PLANNED,)),
            ],
        ),
        name="grad_blocks",
    )(owners, *operands)


def reduce_blocks(halves):
    wide, narrow = (jnp.float32, jnp.bfloat16)
    keep, give = halves
    from_core = send(give, CORE)
    from_far = send((keep[2:].astype(wide) + from_core[2:].astype(wide)).astype(narrow), FAR)
    near_total = (
        keep[1].astype(wide) + from_core[1].astype(wide) + from_far[1].astype(wide)
    ).astype(narrow)
    from_near = send(near_total, NEAR)
    column = (
        keep[0].astype(wide)
        + from_core[0].astype(wide)
        + from_far[0].astype(wide)
        + from_near.astype(wide)
    )
    third = column[3] + send(column[3].astype(narrow), Z_IN).astype(wide)
    second = column[2] + send(column[2].astype(narrow), Z_IN).astype(wide)
    first = column[1] + send(third.astype(narrow), Z_MIDDLE).astype(wide)
    own = column[0] + send(second.astype(narrow), Z_MIDDLE).astype(wide)
    return own + send(first.astype(narrow), Z_PAIR).astype(wide)


def vector_columns(vectors, rows):
    return jnp.concatenate([vector.reshape(rows, -1) for vector in vectors], axis=1)


def planned_step(images, cotangent, live_slots, params):
    (
        ln1_gain,
        ln1_shift,
        w_qkv,
        q_bias,
        v_bias,
        w_out,
        out_bias,
        ln2_gain,
        ln2_shift,
        w_up,
        up_bias,
        w_down,
        down_bias,
    ) = params
    owners = jnp.asarray(owner_table())[lax.axis_index(AXIS)]
    shard = w_qkv.shape[0]
    fan = up_bias.shape[0] // shard
    vectors = (ln1_gain, ln1_shift, q_bias, v_bias, out_bias, ln2_gain, ln2_shift, down_bias, up_bias)
    count = 8 + fan
    columns = jnp.pad(vector_columns(vectors, shard), ((0, 0), (0, 128 - count)))
    qkv_width = w_qkv.shape[1]
    first = assemble(gather_blocks(jnp.concatenate([w_qkv, columns], axis=1)), owners)
    full_out = assemble(gather_blocks(w_out), owners)
    full_up = assemble(gather_blocks(w_up), owners)
    full_down = assemble(gather_blocks(w_down), owners)
    full_columns = first[:, qkv_width : qkv_width + count]
    full_vectors = [full_columns[:, place] for place in range(8)]
    full_up_bias = full_columns[:, 8:].reshape(-1)
    weights = (
        full_vectors[0],
        full_vectors[1],
        first[:, :qkv_width],
        full_vectors[2],
        full_vectors[3],
        full_out,
        full_vectors[4],
        full_vectors[5],
        full_vectors[6],
        full_up,
        full_up_bias,
        full_down,
        full_vectors[7],
    )
    block_out, saved_state = layer_forward(weights, images, live_slots)
    grad_input, grads = layer_backward(weights, saved_state, cotangent, products=True)
    down_total = reduce_blocks(grad_blocks(owners, *grads[11]))
    up_total = reduce_blocks(grad_blocks(owners, *grads[9]))
    out_total = reduce_blocks(grad_blocks(owners, *grads[5]))
    width = grads[0].shape[0]
    grad_vectors = [grads[place] for place in (0, 1, 3, 4, 6, 7, 8, 12, 10)]
    extra = jnp.pad(vector_columns(grad_vectors, width), ((0, 0), (0, 128 - count)))
    extra = extra.astype(jnp.bfloat16).reshape(PLANNED, shard, 128)
    qkv_total = reduce_blocks(grad_blocks(owners, *grads[2], extra))
    vector_totals = [qkv_total[:, qkv_width + place] for place in range(8)]
    up_bias_total = qkv_total[:, qkv_width + 8 : qkv_width + count].reshape(-1)
    return (
        block_out,
        grad_input,
        vector_totals[0],
        vector_totals[1],
        qkv_total[:, :qkv_width],
        vector_totals[2],
        vector_totals[3],
        out_total,
        vector_totals[4],
        vector_totals[5],
        vector_totals[6],
        up_total,
        up_bias_total,
        down_total,
        vector_totals[7],
    )


def on_device(
    images,
    cotangent,
    image_count,
    ln1_gain,
    ln1_shift,
    w_qkv,
    q_bias,
    v_bias,
    w_out,
    out_bias,
    ln2_gain,
    ln2_shift,
    w_up,
    up_bias,
    w_down,
    down_bias,
):
    live_count = image_count[0]
    slot_total = images.shape[0]
    live_slots = jnp.arange(slot_total, dtype=jnp.int32) < live_count
    if lax.axis_size("fsdp") == PLANNED:
        params = (
            ln1_gain,
            ln1_shift,
            w_qkv,
            q_bias,
            v_bias,
            w_out,
            out_bias,
            ln2_gain,
            ln2_shift,
            w_up,
            up_bias,
            w_down,
            down_bias,
        )
        return planned_step(images, cotangent, live_slots, params)
    weights = (
        lax.all_gather(ln1_gain, "fsdp", axis=0, tiled=True),
        lax.all_gather(ln1_shift, "fsdp", axis=0, tiled=True),
        lax.all_gather(w_qkv, "fsdp", axis=0, tiled=True),
        lax.all_gather(q_bias, "fsdp", axis=0, tiled=True),
        lax.all_gather(v_bias, "fsdp", axis=0, tiled=True),
        lax.all_gather(w_out, "fsdp", axis=0, tiled=True),
        lax.all_gather(out_bias, "fsdp", axis=0, tiled=True),
        lax.all_gather(ln2_gain, "fsdp", axis=0, tiled=True),
        lax.all_gather(ln2_shift, "fsdp", axis=0, tiled=True),
        lax.all_gather(w_up, "fsdp", axis=0, tiled=True),
        lax.all_gather(up_bias, "fsdp", axis=0, tiled=True),
        lax.all_gather(w_down, "fsdp", axis=0, tiled=True),
        lax.all_gather(down_bias, "fsdp", axis=0, tiled=True),
    )
    block_out, saved_state = layer_forward(weights, images, live_slots)
    back_weights = (
        lax.all_gather(ln1_gain, "fsdp", axis=0, tiled=True),
        lax.all_gather(ln1_shift, "fsdp", axis=0, tiled=True),
        lax.all_gather(w_qkv, "fsdp", axis=0, tiled=True),
        lax.all_gather(q_bias, "fsdp", axis=0, tiled=True),
        lax.all_gather(v_bias, "fsdp", axis=0, tiled=True),
        lax.all_gather(w_out, "fsdp", axis=0, tiled=True),
        lax.all_gather(out_bias, "fsdp", axis=0, tiled=True),
        lax.all_gather(ln2_gain, "fsdp", axis=0, tiled=True),
        lax.all_gather(ln2_shift, "fsdp", axis=0, tiled=True),
        lax.all_gather(w_up, "fsdp", axis=0, tiled=True),
        lax.all_gather(up_bias, "fsdp", axis=0, tiled=True),
        lax.all_gather(w_down, "fsdp", axis=0, tiled=True),
        lax.all_gather(down_bias, "fsdp", axis=0, tiled=True),
    )
    grad_input, weight_grads = layer_backward(back_weights, saved_state, cotangent)
    grad_shards = owner_sums(weight_grads)
    return (
        block_out,
        grad_input,
        grad_shards[0],
        grad_shards[1],
        grad_shards[2],
        grad_shards[3],
        grad_shards[4],
        grad_shards[5],
        grad_shards[6],
        grad_shards[7],
        grad_shards[8],
        grad_shards[9],
        grad_shards[10],
        grad_shards[11],
        grad_shards[12],
    )


def solution(mesh):
    in_specs = (
        P("fsdp", None, None),
        P("fsdp", None, None),
        P("fsdp"),
        P("fsdp"),
        P("fsdp"),
        P("fsdp", None),
        P("fsdp"),
        P("fsdp"),
        P("fsdp", None),
        P("fsdp"),
        P("fsdp"),
        P("fsdp"),
        P("fsdp", None),
        P("fsdp"),
        P("fsdp", None),
        P("fsdp"),
    )
    out_specs = (
        P("fsdp", None, None),
        P("fsdp", None, None),
        P("fsdp"),
        P("fsdp"),
        P("fsdp", None),
        P("fsdp"),
        P("fsdp"),
        P("fsdp", None),
        P("fsdp"),
        P("fsdp"),
        P("fsdp"),
        P("fsdp", None),
        P("fsdp"),
        P("fsdp", None),
        P("fsdp"),
    )
    return jax.shard_map(
        on_device, mesh=mesh, in_specs=in_specs, out_specs=out_specs, check_vma=False
    )
```
